1024 devices in a mesh: band: 16 (over z_hi, x, core), pw: 64 (over z_lo, y).
Axes of the slice: x: 4, y: 4, z: 32 (z_hi: 2, z_lo: 16; z = z_hi * 16 + z_lo), core: 2. Of those that a mesh axis runs over, the one named last changes fastest.
Arguments:
- coeffs: bfloat16 [2, 64, 8192, 256], P(None, None, ('band', 'pw')), may hold values from -6 to 6
- rotation_matrix: bfloat16 [2, 64, 32], replicated, may hold values from -0.5 to 0.5
- stick_length: int32 [8192], replicated, may hold values from 64 to 256
- stick_column: int32 [8192], replicated, may hold values from 0 to 65535, as said below
- plane_index: int32 [128], replicated, may hold values from 0 to 255, as said below
- occupation: int32 [32], P('band'), may hold values from 0 to 2
Outputs:
- density: float32 [128, 256, 256], P('pw')
The draws below stay inside these ranges and needn't reach their ends.
Inputs may be any that keep to these rules, and one draw needn't show every extreme that they name: `stick_column`: distinct column numbers. `plane_index`: distinct plane numbers.
All inputs are finite; a program needn't handle non-finite values.
Results may differ from the reference program's by a relative error of at most 0.003.
Values may be sent and summed in bfloat16 or wider, within the bound.
A program may use at most 64 MiB of HBM per device.

```python
import math
import jax
import jax.numpy as jnp
from jax import lax

GRID = 256
IN_BANDS = 64
OUT_BANDS = 32
STICKS = 8192
Z_WIN = 128
N_BAND = 16


def draw_stick_column(key, part):
    seeded = jax.random.fold_in(key, 11)
    return jax.random.permutation(seeded, GRID * GRID)[:STICKS].astype(jnp.int32)


def draw_plane_index(key, part):
    seeded = jax.random.fold_in(key, 23)
    return jax.random.permutation(seeded, GRID)[:Z_WIN].astype(jnp.int32)


def set_ends(drawn, rng, low, high):
    longest = drawn.shape.index(max(drawn.shape))
    spots = []
    for shift in (0, 1):
        where = [jax.random.randint(jax.random.fold_in(rng, axis), (), 0, length) for axis, length in enumerate(drawn.shape)]
        where[longest] = (where[longest] + shift) % drawn.shape[longest]
        spots.append(tuple(where))
    return drawn.at[spots[0]].set(low).at[spots[1]].set(high)


def levels(rng, extent, pieces, low, high):
    level, own = 1.0, jax.random.fold_in(rng, 6)
    for axis_at, blocks in pieces:
        heights = jnp.exp(jax.random.uniform(jax.random.fold_in(own, axis_at), (blocks,), jnp.float32, low / len(pieces), high / len(pieces)))
        level = level * jnp.repeat(heights, extent[axis_at] // blocks).reshape([-1 if axis == axis_at else 1 for axis in range(len(extent))])
    return level


def scatter_about(rng, dims, width, bound, cuts=(), kind=jnp.bfloat16):
    values = width * jax.random.normal(rng, dims, jnp.float32)
    if cuts:
        values = values * levels(rng, dims, cuts, -0.22, 0.18)
    return jnp.clip(values, -bound, bound).astype(kind)


def setup_inputs(seed: int = 0) -> dict:
    streams_of = jax.random.split(jax.random.key(seed), 7)
    return {
        "coeffs": scatter_about(streams_of[0], (2, IN_BANDS, STICKS, GRID), 1.0, 6.0, ((2, 1024),)),
        "rotation_matrix": scatter_about(streams_of[1], (2, IN_BANDS, OUT_BANDS), (2 * IN_BANDS) ** -0.5, 0.5),
        "stick_length": set_ends(jax.random.randint(streams_of[2], (STICKS,), GRID // 4, GRID + 1), jax.random.fold_in(streams_of[2], 1), GRID // 4, GRID).astype(jnp.int32),
        "stick_column": draw_stick_column(jax.random.fold_in(streams_of[6], 71), 0),
        "plane_index": draw_plane_index(jax.random.fold_in(streams_of[6], 71), 0),
        "occupation": set_ends(jax.random.randint(streams_of[5], (OUT_BANDS,), 0, 3), jax.random.fold_in(streams_of[5], 1), 0, 2).astype(jnp.int32),
    }


def tables(grid_len, indices):
    product = (jnp.arange(grid_len, dtype=jnp.int32)[:, None] * indices[None, :]) % grid_len
    angles = (2.0 * math.pi / grid_len) * product.astype(jnp.float32)
    return jnp.cos(angles).astype(jnp.bfloat16), jnp.sin(angles).astype(jnp.bfloat16)


def contract(form, left, right):
    return jnp.einsum(form, left.astype(jnp.float32), right.astype(jnp.float32), precision=lax.Precision.HIGHEST)


def rotate(coeff_part, rotation_matrix):
    in_count = rotation_matrix.shape[1]
    out_count = rotation_matrix.shape[2]
    rotation = jnp.concatenate([jnp.concatenate([rotation_matrix[0], rotation_matrix[1]], 1), jnp.concatenate([-rotation_matrix[1], rotation_matrix[0]], 1)], 0)
    flattened = coeff_part.reshape(2 * in_count, -1)
    result = jnp.dot(rotation.T, flattened, preferred_element_type=jnp.float32)
    return result.reshape((2, out_count) + coeff_part.shape[2:]).astype(jnp.bfloat16)


def z_transform(rotated, lengths, plane_index):
    grid_len = rotated.shape[3]
    count = plane_index.shape[0]
    live_mask = (jnp.arange(grid_len, dtype=jnp.int32)[None, :] < lengths[:, None]).astype(jnp.bfloat16)
    masked = rotated * live_mask
    cos_table, sin_table = tables(grid_len, plane_index)
    weight = jnp.concatenate([jnp.concatenate([cos_table, sin_table], 1), jnp.concatenate([-sin_table, cos_table], 1)], 0)
    stacked = jnp.concatenate([masked[0], masked[1]], axis=-1)
    amplitude = contract('bsj,jk->bsk', stacked, weight)
    amp_real = amplitude[..., :count]
    amp_imag = amplitude[..., count:]
    shift = ((lengths // 2)[:, None] * plane_index[None, :]) % grid_len
    phase = (-2.0 * math.pi / grid_len) * shift.astype(jnp.float32)
    phase_cos = jnp.cos(phase)
    phase_sin = jnp.sin(phase)
    out_real = amp_real * phase_cos - amp_imag * phase_sin
    out_imag = amp_real * phase_sin + amp_imag * phase_cos
    result = jnp.stack([out_real, out_imag])
    return jnp.swapaxes(result, 2, 3).astype(jnp.bfloat16)


def plane_power(values, columns, grid_len):
    shape = values.shape
    flattened = jnp.zeros(shape[:3] + (grid_len * grid_len,), jnp.bfloat16).at[..., columns].set(values)
    planes = flattened.reshape(shape[:3] + (grid_len, grid_len))
    cos_table, sin_table = tables(grid_len, jnp.arange(grid_len, dtype=jnp.int32))
    half_real = (contract('bzxy,yk->bzxk', planes[0], cos_table) - contract('bzxy,yk->bzxk', planes[1], sin_table)).astype(jnp.bfloat16)
    half_imag = (contract('bzxy,yk->bzxk', planes[0], sin_table) + contract('bzxy,yk->bzxk', planes[1], cos_table)).astype(jnp.bfloat16)
    wave_real = contract('xq,bzxk->bzqk', cos_table, half_real) - contract('xq,bzxk->bzqk', sin_table, half_imag)
    wave_imag = contract('xq,bzxk->bzqk', sin_table, half_real) + contract('xq,bzxk->bzqk', cos_table, half_imag)
    return wave_real * wave_real + wave_imag * wave_imag


def reference(coeffs, rotation_matrix, stick_length, stick_column, plane_index, occupation):
    block_len = STICKS // N_BAND

    def one_group(group):
        first_row = (group * block_len).astype(jnp.int32)
        coeff_part = lax.dynamic_slice_in_dim(coeffs, first_row, block_len, 2)
        lengths = lax.dynamic_slice_in_dim(stick_length, first_row, block_len, 0)
        return z_transform(rotate(coeff_part, rotation_matrix), lengths, plane_index)

    grouped = lax.map(one_group, jnp.arange(N_BAND, dtype=jnp.int32))
    z_values = jnp.transpose(grouped, (1, 2, 3, 0, 4)).reshape(2, OUT_BANDS, Z_WIN, STICKS)
    by_plane = jnp.moveaxis(z_values, 2, 0)
    weights = occupation.astype(jnp.float32)

    def one_plane(values):
        power = plane_power(values[:, :, None, :], stick_column, GRID)[:, 0]
        return jnp.einsum('b,bxy->xy', weights, power)

    total = lax.map(one_plane, by_plane)
    return total / jnp.float32(OUT_BANDS * STICKS * GRID)
```

```python
import functools
import math

import jax
import jax.numpy as jnp
from jax import lax
from jax.experimental import pallas as pl
from jax.experimental.pallas import tpu as pltpu
from jax.sharding import PartitionSpec as P

MESH = pl.DeviceIdType.MESH
GRID = 256
NZ = 32
NI = 8
NQ = 32
STICK = 8
VALS = 8
VMEM_LIMIT = 60 * 1024 * 1024


def place():
    band = lax.axis_index("band")
    pw = lax.axis_index("pw")
    z = band // NI * 16 + pw // 4
    return z, pw % 4, band % NI


def device(z, y, i):
    return (z // 16 * NI + i, z % 16 * 4 + y)


def parity(z):
    return (z + 24) % NZ // 16


def exchange_kernel(send, out, recv, staged, s1, r1, s2, r2, own):
    z, y, i = place()
    q = y * NI + i

    def near(t):
        return device(z, t // NI, t % NI)

    def far(t):
        return device(t, y, i)

    barrier = pltpu.get_barrier_semaphore()

    @pl.loop(1, NZ)
    def _(p):
        pl.semaphore_signal(barrier, inc=1, device_id=far((z + p) % NZ), device_id_type=MESH)

    @pl.loop(1, NQ)
    def _(p):
        pl.semaphore_signal(barrier, inc=1, device_id=near((q + p) % NQ), device_id_type=MESH)

    pl.semaphore_wait(barrier, NZ + NQ - 2)

    def first(slot_src, slot_dst, sem_send, sem_recv, target):
        return pltpu.make_async_remote_copy(
            src_ref=send.at[slot_src],
            dst_ref=recv.at[slot_dst],
            send_sem=s1.at[sem_send],
            recv_sem=r1.at[sem_recv],
            device_id=target,
            device_id_type=MESH,
        )

    def second(slot_src, slot_dst, sem_send, sem_recv, target):
        return pltpu.make_async_remote_copy(
            src_ref=staged.at[slot_src],
            dst_ref=out.at[slot_dst],
            send_sem=s2.at[sem_send],
            recv_sem=r2.at[sem_recv],
            device_id=target,
            device_id_type=MESH,
        )

    @pl.loop(1, NQ)
    def _(p):
        t = (q + p) % NQ
        first(t, q, t, q, near(t)).start()

    local = pltpu.make_async_copy(send.at[q], recv.at[q], own.at[0])
    local.start()
    local.wait()

    @pl.loop(1, NQ)
    def _(p):
        t = (q + NQ - p) % NQ
        first(t, t, t, t, near(t)).wait_recv()

    turned = jnp.swapaxes(recv[...].astype(jnp.float32), 0, 1)
    low, high = turned[:, :16], turned[:, 16:]
    left = lax.broadcasted_iota(jnp.int32, low.shape, 2) < 64
    staged[0:16] = jnp.where(left, low, pltpu.roll(high, 64, 2)).astype(jnp.bfloat16)
    staged[16:32] = jnp.where(left, pltpu.roll(low, 64, 2), high).astype(jnp.bfloat16)

    @pl.loop(1, NZ)
    def _(p):
        t = (z + (16 + p // 2 * (1 - p % 2 * 2))) % NZ
        second(t, z, t, z, far(t)).start()

    local2 = pltpu.make_async_copy(staged.at[z], out.at[z], own.at[1])
    local2.start()
    local2.wait()

    @pl.loop(1, NZ)
    def _(p):
        t = (z + NZ - p) % NZ
        second(t, t, t, t, far(t)).wait_recv()

    @pl.loop(1, NQ)
    def _(p):
        t = (q + p) % NQ
        first(t, t, t, t, near(t)).wait_send()

    @pl.loop(1, NZ)
    def _(p):
        t = (z + p) % NZ
        second(t, t, t, t, far(t)).wait_send()


def exchange(tiles):
    return pl.pallas_call(
        exchange_kernel,
        out_shape=jax.ShapeDtypeStruct((NZ, 16, 128), jnp.bfloat16),
        in_specs=[pl.BlockSpec(memory_space=pltpu.VMEM)],
        out_specs=pl.BlockSpec(memory_space=pltpu.VMEM),
        scratch_shapes=[
            pltpu.VMEM((NQ, 16, 128), jnp.bfloat16),
            pltpu.VMEM((NZ, 16, 128), jnp.bfloat16),
            pltpu.SemaphoreType.DMA((NQ,)),
            pltpu.SemaphoreType.DMA((NQ,)),
            pltpu.SemaphoreType.DMA((NZ,)),
            pltpu.SemaphoreType.DMA((NZ,)),
            pltpu.SemaphoreType.DMA((2,)),
        ],
        compiler_params=pltpu.CompilerParams(collective_id=1, has_side_effects=True),
        name="exchange",
    )(tiles)


def planes_kernel(scale, weight, vals, xs, ys, table, dens, rows, spread, total, half):
    flat = vals[...].reshape(NZ * 16, 128).astype(jnp.float32).T
    for h in range(2):
        part = flat[h * 64 : h * 64 + 64].reshape(VALS, STICK, NZ * 16)
        rows[:, :, h * 512 : h * 512 + 512] = jnp.swapaxes(part, 0, 1).astype(jnp.bfloat16)
    count = rows.shape[2]

    def gather(s, _):
        grid_at = lax.broadcasted_iota(jnp.int32, (GRID, count), 0)
        hit_x = jnp.where(grid_at == xs[pl.ds(s, 1), :], 1.0, 0.0).astype(jnp.bfloat16)
        hit_y = jnp.where(grid_at == ys[pl.ds(s, 1), :], 1.0, 0.0).astype(jnp.bfloat16)
        value = rows[s]
        for v in range(VALS):
            spread[v * GRID : (v + 1) * GRID, :] = hit_y * value[v : v + 1, :]
        product = lax.dot_general(
            spread[...], hit_x, (((1,), (1,)), ((), ())), preferred_element_type=jnp.float32
        )

        @pl.when(s == 0)
        def _():
            total[...] = product

        @pl.when(s != 0)
        def _():
            total[...] += product

        return 0

    lax.fori_loop(0, STICK, gather, 0)
    for b in range(4):
        real = total[b * GRID : (b + 1) * GRID, :]
        imag = total[(4 + b) * GRID : (5 + b) * GRID, :]
        plane = jnp.concatenate([real, imag], 0).astype(jnp.bfloat16)
        mid = jnp.dot(table[...], plane, preferred_element_type=jnp.float32).astype(jnp.bfloat16)
        half[:, 0:GRID] = mid[0:GRID]
        half[:, GRID : 2 * GRID] = mid[GRID : 2 * GRID]
        wave = lax.dot_general(
            table[...], half[...], (((1,), (1,)), ((), ())), preferred_element_type=jnp.float32
        )
        power = wave[0:GRID] * wave[0:GRID] + wave[GRID:] * wave[GRID:]
        term = power * (weight[b].astype(jnp.float32) * scale)
        if b == 0:
            dens[...] = term
        else:
            dens[...] += term


def planes(weight, vals, xs, ys, table, scale):
    vmem = pl.BlockSpec(memory_space=pltpu.VMEM)
    return pl.pallas_call(
        functools.partial(planes_kernel, scale),
        out_shape=jax.ShapeDtypeStruct((GRID, GRID), jnp.float32),
        in_specs=[pl.BlockSpec(memory_space=pltpu.SMEM)] + [vmem] * 4,
        out_specs=vmem,
        scratch_shapes=[
            pltpu.VMEM((STICK, VALS, NZ * NQ), jnp.bfloat16),
            pltpu.VMEM((VALS * GRID, NZ * NQ), jnp.bfloat16),
            pltpu.VMEM((VALS * GRID, GRID), jnp.float32),
            pltpu.VMEM((GRID, 2 * GRID), jnp.bfloat16),
        ],
        compiler_params=pltpu.CompilerParams(vmem_limit_bytes=VMEM_LIMIT),
        name="planes",
    )(weight, vals, xs, ys, table)


def collect_kernel(part, out, shares, mine, held, full, s1, r1, s2, r2, s3, r3):
    z, y, i = place()
    slot = parity(z)
    up, down = (z + 8) % NZ, (z + 24) % NZ
    barrier = pltpu.get_barrier_semaphore()
    for t in (up, down):
        pl.semaphore_signal(barrier, inc=1, device_id=device(t, y, i), device_id_type=MESH)

    @pl.loop(1, NI)
    def _(p):
        pl.semaphore_signal(
            barrier, inc=1, device_id=device(z, y, (i + p) % NI), device_id_type=MESH
        )

    pl.semaphore_wait(barrier, NI + 1)

    def share(src, dst, t):
        return pltpu.make_async_remote_copy(
            src_ref=part.at[src],
            dst_ref=shares.at[dst],
            send_sem=s1.at[src],
            recv_sem=r1.at[dst],
            device_id=device(z, y, t),
            device_id_type=MESH,
        )

    @pl.loop(1, NI)
    def _(p):
        t = (i + p) % NI
        share(t, i, t).start()

    @pl.loop(1, NI)
    def _(p):
        t = (i + NI - p) % NI
        share(t, t, t).wait_recv()

    shares[i] = part[i]
    total = shares[0]
    for t in range(1, NI):
        total = total + shares[t]
    mine[...] = total.astype(jnp.bfloat16)

    def hop(which, at, t):
        return pltpu.make_async_remote_copy(
            src_ref=mine,
            dst_ref=held.at[at],
            send_sem=s2.at[which],
            recv_sem=r2.at[at],
            device_id=device(t, y, i),
            device_id_type=MESH,
        )

    hop(0, slot, up).start()
    hop(1, slot, down).start()

    def spread(k, src, t):
        return pltpu.make_async_remote_copy(
            src_ref=held.at[k],
            dst_ref=full.at[k, src],
            send_sem=s3.at[k, t],
            recv_sem=r3.at[k, src],
            device_id=device(z, y, t),
            device_id_type=MESH,
        )

    for k in range(2):
        hop(0, k, up).wait_recv()

        @pl.loop(1, NI)
        def _(p):
            t = (i + p) % NI
            spread(k, i, t).start()

        out[k, i] = held[k].astype(jnp.float32)

    for k in range(2):

        @pl.loop(1, NI)
        def _(p):
            t = (i + NI - p) % NI
            spread(k, t, t).wait_recv()
            out[k, t] = full[k, t].astype(jnp.float32)

    hop(0, slot, up).wait_send()
    hop(1, slot, down).wait_send()

    @pl.loop(1, NI)
    def _(p):
        t = (i + p) % NI
        share(t, t, t).wait_send()
        for k in range(2):
            spread(k, t, t).wait_send()


def collect(part):
    height = GRID // NI
    vmem = pl.BlockSpec(memory_space=pltpu.VMEM)
    dma = pltpu.SemaphoreType.DMA
    result = pl.pallas_call(
        collect_kernel,
        out_shape=jax.ShapeDtypeStruct((2, NI, height, GRID), jnp.float32),
        in_specs=[vmem],
        out_specs=vmem,
        scratch_shapes=[
            pltpu.VMEM((NI, height, GRID), jnp.float32),
            pltpu.VMEM((height, GRID), jnp.bfloat16),
            pltpu.VMEM((2, height, GRID), jnp.bfloat16),
            pltpu.VMEM((2, NI, height, GRID), jnp.bfloat16),
            dma((NI,)),
            dma((NI,)),
            dma((2,)),
            dma((2,)),
            dma((2, NI)),
            dma((2, NI)),
        ],
        compiler_params=pltpu.CompilerParams(collective_id=2, has_side_effects=True),
        name="collect",
    )(part.reshape(NI, height, GRID))
    return result.reshape(2, GRID, GRID)


def angles(product):
    return 2.0 * math.pi / GRID * (product % GRID).astype(jnp.float32)


def transform(coeffs, rotation_matrix, lengths, planes_at):
    real, imag = rotation_matrix[0], rotation_matrix[1]
    to_real = jnp.concatenate([real, -imag], 0).T
    to_imag = jnp.concatenate([imag, real], 0).T
    forms = jnp.stack([to_real, -to_imag, to_imag, to_real, -to_imag, -to_real, to_real, -to_imag])
    forms = forms.reshape(2, 2, 2, 2, NI, 2, 128)
    forms = jnp.transpose(forms, (0, 4, 1, 3, 5, 2, 6))
    rotated = jnp.einsum(
        "ok,ksj->osj",
        forms.reshape(2 * NI * VALS * 2, 128),
        coeffs.reshape(128, STICK, GRID),
        preferred_element_type=jnp.float32,
    ).astype(jnp.bfloat16)
    at = jnp.arange(GRID, dtype=jnp.int32)
    live = (at[None, :] < lengths[:, None]).astype(jnp.bfloat16)
    masked = (rotated * live).reshape(2, NI * VALS, 2, STICK, GRID)
    turn = angles(planes_at[:, None] * at[None, :])
    waves = jnp.stack([jnp.cos(turn), jnp.sin(turn)], 1).astype(jnp.bfloat16)
    amplitude = jnp.einsum("ktj,gntsj->gkns", waves, masked, preferred_element_type=jnp.float32)
    phase = -angles(planes_at[:, None] * (lengths // 2)[None, :])[:, None, :]
    values = amplitude[0] * jnp.cos(phase) + amplitude[1] * jnp.sin(phase)
    values = values.astype(jnp.bfloat16).reshape(2, 4, 16, NI, VALS * STICK)
    return jnp.transpose(values, (1, 3, 2, 0, 4)).reshape(NQ, 16, 128)


def shards(coeffs, rotation_matrix, stick_length, stick_column, plane_index, occupation):
    band_count = lax.axis_size("band")
    z, y, i = place()
    row = lax.axis_index("band") * lax.axis_size("pw") + lax.axis_index("pw")
    lengths = lax.dynamic_slice_in_dim(stick_length, row * STICK, STICK)
    by_group = plane_index.reshape(16, 4, 2)
    lower, upper = by_group[0:8], by_group[8:16]
    ordered = jnp.stack(
        [
            jnp.concatenate([upper[:, :, 1], lower[:, :, 0]], 0).T,
            jnp.concatenate([upper[:, :, 0], lower[:, :, 1]], 0).T,
        ]
    )
    tiles = transform(coeffs, rotation_matrix, lengths, ordered.reshape(-1))
    received = exchange(tiles)
    column = jnp.transpose(stick_column.reshape(2, NI, 16, 2, 2, STICK), (3, 5, 0, 2, 4, 1))
    column = jnp.transpose(column.reshape(2, STICK, 512), (1, 0, 2)).reshape(STICK, 1024)
    pair = [(b, (b + NI) % band_count) for b in range(band_count)]
    other = lax.ppermute(occupation, "band", pair)
    low = z < 16
    weight = jnp.concatenate(
        [jnp.where(low, occupation, other), jnp.where(low, other, occupation)]
    )
    at = jnp.arange(GRID, dtype=jnp.int32)
    turn = angles(at[:, None] * at[None, :])
    cos_table = jnp.cos(turn).astype(jnp.bfloat16)
    sin_table = jnp.sin(turn).astype(jnp.bfloat16)
    table = jnp.concatenate(
        [
            jnp.concatenate([cos_table, -sin_table], 1),
            jnp.concatenate([sin_table, cos_table], 1),
        ],
        0,
    )
    scale = 1.0 / float(occupation.shape[0] * band_count * stick_column.shape[0] * GRID)
    part = planes(weight, received, column // GRID, column % GRID, table, scale)
    return collect(part)


def solution(mesh):
    return jax.shard_map(
        shards,
        mesh=mesh,
        in_specs=(P(None, None, ("band", "pw"), None), P(), P(), P(), P(), P("band")),
        out_specs=P("pw", None, None),
        check_vma=False,
    )
```

```python
import math

import jax
import jax.numpy as jnp
import numpy as np
from jax import lax
from jax.experimental import pallas as pl
from jax.experimental.pallas import tpu as pltpu
from jax.sharding import PartitionSpec as P

MESH = pl.DeviceIdType.MESH
GRID = 256
NZ = 32
NI = 8
NQ = 32
STICK = 8
VALS = 8
OCTET = 8 * 16 * 16
HIGH = GRID // NI
VMEM_LIMIT = 62 * 1024 * 1024
ACROSS = (((1,), (1,)), ((), ()))


def place():
    band = lax.axis_index("band")
    pw = lax.axis_index("pw")
    z = band // NI * 16 + pw // 4
    return z, pw % 4, band % NI


def device(z, y, i):
    return (z // 16 * NI + i, z % 16 * 4 + y)


def parity(z):
    return (z + 24) % NZ // 16


def fourier():
    at = np.arange(GRID)
    turn = np.float32(2.0 * math.pi / GRID) * (at[:, None] * at[None, :] % GRID).astype(np.float32)
    cos, sin = np.cos(turn), np.sin(turn)
    return np.concatenate([np.concatenate([cos, -sin], 1), np.concatenate([sin, cos], 1)], 0)


def band_choice():
    choice = np.zeros((2, NI, 2, 4, 2, 32), np.float32)
    for i in range(NI):
        for k in range(4):
            b = k // 2 * 16 + 2 * i + k % 2
            choice[0, i, 0, k, 0, b] = 1.0
            choice[0, i, 1, k, 1, b] = 1.0
            choice[1, i, 0, k, 1, b] = 1.0
            choice[1, i, 1, k, 0, b] = -1.0
    return choice.reshape(128, 64)


def plane_order():
    order = np.zeros((2, 4, 16, 128), np.float32)
    for high in range(2):
        for y in range(4):
            for low in range(16):
                k = 2 * ((low + 8) % 16 * 4 + y) + parity(high * 16 + low)
                order[high, y, low, k] = 1.0
    return order.reshape(128, 128)


def dot(a, b):
    return jnp.dot(a, b, preferred_element_type=jnp.float32)


def dot_across(a, b):
    return lax.dot_general(a, b, ACROSS, preferred_element_type=jnp.float32)


def narrow(a):
    return a.astype(jnp.bfloat16)


def wide(a):
    return a.astype(jnp.float32)


def kernel(
    scale,
    coeffs,
    rotation,
    live,
    phase,
    picked,
    xs,
    ys,
    share_own,
    table,
    choice,
    order,
    out,
    send,
    recv,
    staged,
    sticks,
    turned,
    spread,
    hits,
    total,
    half,
    part,
    shares,
    mine,
    held,
    share_other,
    s1,
    r1,
    s2,
    r2,
    s3,
    r3,
    s4,
    r4,
    s5,
    r5,
    own,
    s6,
    r6,
):
    z, y, i = place()
    q = y * NI + i

    def near(t):
        return device(z, t // NI, t % NI)

    def far(t):
        return device(t, y, i)

    barrier = pltpu.get_barrier_semaphore()

    @pl.loop(1, NZ)
    def _(p):
        pl.semaphore_signal(barrier, inc=1, device_id=far((z + p) % NZ), device_id_type=MESH)

    @pl.loop(1, NQ)
    def _(p):
        pl.semaphore_signal(barrier, inc=1, device_id=near((q + p) % NQ), device_id_type=MESH)

    by_stick = narrow(jnp.swapaxes(wide(coeffs[...]), 0, 1))
    forms = narrow(dot_across(choice[...], rotation[...]))
    for s in range(STICK):
        rotated = wide(narrow(dot(forms, by_stick[s])) * live[s : s + 1, :])
        for t in range(2):
            turned[:, s, :, t * GRID : (t + 1) * GRID] = rotated[t * 64 : t * 64 + 64].reshape(
                NI, VALS, GRID
            )
    rows = narrow(turned[...].reshape(NI * STICK * VALS, 2 * GRID))
    waves0 = narrow(dot(picked[...], table[0:GRID, :]))
    waves1 = narrow(dot(picked[...], table[GRID : 2 * GRID, :]))
    cos = jnp.concatenate([phase[0]] * 4, 1)
    sin = jnp.concatenate([phase[1]] * 4, 1)
    values = dot_across(waves0, rows) * cos + dot_across(waves1, rows) * sin
    values = dot(order[...], narrow(values))
    left = lax.broadcasted_iota(jnp.int32, (16, 128), 1) < 64
    for b in range(4):
        for pair in range(4):
            lower = values[b * 16 : b * 16 + 16, pair * 128 : pair * 128 + 128]
            upper = values[64 + b * 16 : 80 + b * 16, pair * 128 : pair * 128 + 128]
            at = b * NI + 2 * pair
            send[at] = narrow(jnp.where(left, lower, pltpu.roll(upper, 64, 1)))
            send[at + 1] = narrow(jnp.where(left, pltpu.roll(lower, 64, 1), upper))

    pl.semaphore_wait(barrier, NZ + NQ - 2)

    def first(slot_src, slot_dst, target):
        return pltpu.make_async_remote_copy(
            src_ref=send.at[slot_src],
            dst_ref=recv.at[slot_dst],
            send_sem=s1.at[slot_src],
            recv_sem=r1.at[slot_dst],
            device_id=target,
            device_id_type=MESH,
        )

    def second(slot_src, slot_dst, target):
        return pltpu.make_async_remote_copy(
            src_ref=staged.at[slot_src],
            dst_ref=sticks.at[slot_dst],
            send_sem=s2.at[slot_src],
            recv_sem=r2.at[slot_dst],
            device_id=target,
            device_id_type=MESH,
        )

    @pl.loop(1, NQ)
    def _(p):
        t = (q + p) % NQ
        first(t, q, near(t)).start()

    weights = pltpu.make_async_remote_copy(
        src_ref=share_own,
        dst_ref=share_other,
        send_sem=s6,
        recv_sem=r6,
        device_id=far((z + 16) % NZ),
        device_id_type=MESH,
    )
    weights.start()
    keep = pltpu.make_async_copy(send.at[q], recv.at[q], own.at[0])
    keep.start()
    keep.wait()

    @pl.loop(1, NQ)
    def _(p):
        t = (q + NQ - p) % NQ
        first(t, t, near(t)).wait_recv()

    swapped = jnp.swapaxes(wide(recv[...]), 0, 1)
    lower, upper = swapped[:, :16], swapped[:, 16:]
    left = lax.broadcasted_iota(jnp.int32, lower.shape, 2) < 64
    staged[0:16] = narrow(jnp.where(left, lower, pltpu.roll(upper, 64, 2)))
    staged[16:32] = narrow(jnp.where(left, pltpu.roll(lower, 64, 2), upper))

    @pl.loop(1, NZ)
    def _(p):
        t = (z + (16 + p // 2 * (1 - p % 2 * 2))) % NZ
        second(t, z, far(t)).start()

    keep2 = pltpu.make_async_copy(staged.at[z], sticks.at[z], own.at[1])
    keep2.start()
    keep2.wait()

    @pl.loop(0, 4)
    def _(step):
        octet = (z // 8 + step + step // 2 - 2 * (step // 3)) % 4

        @pl.loop(0, 8)
        def _(p):
            t = octet * 8 + p

            @pl.when(t != z)
            def _():
                second(t, t, far(t)).wait_recv()

        block = wide(sticks[pl.ds(octet * 8, 8)].reshape(128, 128)).T
        held_rows = block.reshape(16, VALS, 128)
        shares_rows = narrow(held_rows)
        for b in range(16):
            grid_at = lax.broadcasted_iota(jnp.int32, (GRID, 128), 0)
            hit_x = narrow(jnp.where(grid_at == xs[octet, b : b + 1, :], 1.0, 0.0))
            hit_y = narrow(jnp.where(grid_at == ys[octet, b : b + 1, :], 1.0, 0.0))
            hits[:, b * 128 : b * 128 + 128] = hit_x
            for v in range(VALS):
                spread[v * GRID : (v + 1) * GRID, b * 128 : b * 128 + 128] = (
                    hit_y * shares_rows[b, v : v + 1, :]
                )

        @pl.loop(0, 4)
        def _(m):
            at = pl.ds(pl.multiple_of(m * 512, 512), 512)
            product = dot_across(spread[at, :], hits[...])

            @pl.when(step == 0)
            def _():
                total[at, :] = product

            @pl.when(step != 0)
            def _():
                total[at, :] += product

    weights.wait_recv()
    low = z < 16
    for b in range(4):
        real = total[b * GRID : (b + 1) * GRID, :]
        imag = total[(4 + b) * GRID : (5 + b) * GRID, :]
        mid = narrow(dot(table[...], narrow(jnp.concatenate([real, imag], 0))))
        half[:, 0:GRID] = mid[0:GRID]
        half[:, GRID : 2 * GRID] = mid[GRID : 2 * GRID]
        wave = dot_across(table[...], half[...])
        power = wave[0:GRID] * wave[0:GRID] + wave[GRID:] * wave[GRID:]
        here, there = share_own[b % 2, 0:1, :], share_other[b % 2, 0:1, :]
        weight = jnp.where(low, here, there) if b < 2 else jnp.where(low, there, here)
        term = power * (jnp.concatenate([weight, weight], 1) * scale)
        term = term.reshape(NI, HIGH, GRID)
        if b == 0:
            part[...] = term
        else:
            part[...] += term

    def share(src, dst, t):
        return pltpu.make_async_remote_copy(
            src_ref=part.at[src],
            dst_ref=shares.at[dst],
            send_sem=s3.at[src],
            recv_sem=r3.at[dst],
            device_id=device(z, y, t),
            device_id_type=MESH,
        )

    @pl.loop(1, NI)
    def _(p):
        t = (i + p) % NI
        share(t, i, t).start()

    shares[i] = part[i]

    @pl.loop(1, NI)
    def _(p):
        t = (i + NI - p) % NI
        share(t, t, t).wait_recv()

    summed = shares[0]
    for t in range(1, NI):
        summed = summed + shares[t]
    mine[...] = narrow(summed)
    slot = parity(z)
    up, down = (z + 8) % NZ, (z + 24) % NZ

    def hop(which, at, t):
        return pltpu.make_async_remote_copy(
            src_ref=mine,
            dst_ref=held.at[at],
            send_sem=s4.at[which],
            recv_sem=r4.at[at],
            device_id=far(t),
            device_id_type=MESH,
        )

    hop(0, slot, up).start()
    hop(1, slot, down).start()

    def spread_out(k, src, t):
        return pltpu.make_async_remote_copy(
            src_ref=held.at[k],
            dst_ref=out.at[k, src],
            send_sem=s5.at[k, t],
            recv_sem=r5.at[k, src],
            device_id=device(z, y, t),
            device_id_type=MESH,
        )

    for k in range(2):
        hop(0, k, up).wait_recv()

        @pl.loop(1, NI)
        def _(p):
            t = (i + p) % NI
            spread_out(k, i, t).start()

        out[k, i] = held[k]

    for k in range(2):

        @pl.loop(1, NI)
        def _(p):
            t = (i + NI - p) % NI
            spread_out(k, t, t).wait_recv()

    weights.wait_send()
    hop(0, slot, up).wait_send()
    hop(1, slot, down).wait_send()

    @pl.loop(1, NI)
    def _(p):
        t = (i + p) % NI
        share(t, t, t).wait_send()
        for k in range(2):
            spread_out(k, t, t).wait_send()

    @pl.loop(1, NQ)
    def _(p):
        t = (q + p) % NQ
        first(t, t, near(t)).wait_send()

    @pl.loop(1, NZ)
    def _(p):
        t = (z + p) % NZ
        second(t, t, far(t)).wait_send()


def shards(coeffs, rotation_matrix, stick_length, stick_column, plane_index, occupation):
    band_count = lax.axis_size("band")
    row = lax.axis_index("band") * lax.axis_size("pw") + lax.axis_index("pw")
    lengths = lax.dynamic_slice_in_dim(stick_length, row * STICK, STICK)
    real, imag = rotation_matrix[0], rotation_matrix[1]
    rotation = jnp.concatenate(
        [jnp.concatenate([real, imag], 1), jnp.concatenate([-imag, real], 1)], 0
    )
    at = jnp.arange(GRID, dtype=jnp.int32)
    live = narrow(at[None, :] < lengths[:, None])
    shift = jnp.broadcast_to((lengths // 2)[None, :, None], (2, STICK, VALS)).reshape(1, 128)
    product = plane_index[:, None] * shift % GRID
    angle = 2.0 * math.pi / GRID * wide(product)
    phase = jnp.stack([jnp.cos(angle), jnp.sin(angle)])
    picked = narrow(plane_index[:, None] == at[None, :])
    column = stick_column.reshape(2, NI, 2, 8, 2, 2, STICK)
    column = jnp.transpose(column, (0, 2, 4, 6, 3, 5, 1)).reshape(4, 16, 128)
    weights = jnp.broadcast_to(wide(occupation)[:, None, None], (2, 8, 128))
    scale = 1.0 / float(occupation.shape[0] * band_count * stick_column.shape[0] * GRID)
    vmem = pl.BlockSpec(memory_space=pltpu.VMEM)
    dma = pltpu.SemaphoreType.DMA
    bf16, f32 = jnp.bfloat16, jnp.float32
    result = pl.pallas_call(
        lambda *refs: kernel(scale, *refs),
        out_shape=jax.ShapeDtypeStruct((2, NI, HIGH, GRID), bf16),
        in_specs=[vmem] * 11,
        out_specs=vmem,
        scratch_shapes=[
            pltpu.VMEM((NQ, 16, 128), bf16),
            pltpu.VMEM((NQ, 16, 128), bf16),
            pltpu.VMEM((NZ, 16, 128), bf16),
            pltpu.VMEM((NZ, 16, 128), bf16),
            pltpu.VMEM((NI, STICK, VALS, 2 * GRID), f32),
            pltpu.VMEM((VALS * GRID, OCTET), bf16),
            pltpu.VMEM((GRID, OCTET), bf16),
            pltpu.VMEM((VALS * GRID, GRID), f32),
            pltpu.VMEM((GRID, 2 * GRID), bf16),
            pltpu.VMEM((NI, HIGH, GRID), f32),
            pltpu.VMEM((NI, HIGH, GRID), f32),
            pltpu.VMEM((HIGH, GRID), bf16),
            pltpu.VMEM((2, HIGH, GRID), bf16),
            pltpu.VMEM((2, 8, 128), f32),
            dma((NQ,)),
            dma((NQ,)),
            dma((NZ,)),
            dma((NZ,)),
            dma((NI,)),
            dma((NI,)),
            dma((2,)),
            dma((2,)),
            dma((2, NI)),
            dma((2, NI)),
            dma((2,)),
            dma,
            dma,
        ],
        compiler_params=pltpu.CompilerParams(
            collective_id=1, has_side_effects=True, vmem_limit_bytes=VMEM_LIMIT
        ),
        name="density",
    )(
        coeffs.reshape(128, STICK, GRID),
        rotation,
        live,
        phase,
        picked,
        column // GRID,
        column % GRID,
        weights,
        jnp.asarray(fourier(), bf16),
        jnp.asarray(band_choice(), bf16),
        jnp.asarray(plane_order(), bf16),
    )
    return wide(result.reshape(2, GRID, GRID))


def solution(mesh):
    return jax.shard_map(
        shards,
        mesh=mesh,
        in_specs=(P(None, None, ("band", "pw"), None), P(), P(), P(), P(), P("band")),
        out_specs=P("pw", None, None),
        check_vma=False,
    )
```

```python
import math

import jax
import jax.numpy as jnp
import numpy as np
from jax import lax
from jax.experimental import pallas as pl
from jax.experimental.pallas import tpu as pltpu
from jax.sharding import PartitionSpec as P

MESH = pl.DeviceIdType.MESH
GRID = 256
NZ = 32
NI = 8
NQ = 32
STICK = 8
VALS = 8
OCTET = 8 * 16 * 16
HIGH = GRID // NI
VMEM_LIMIT = 62 * 1024 * 1024
ACROSS = (((1,), (1,)), ((), ()))


def place():
    band = lax.axis_index("band")
    pw = lax.axis_index("pw")
    z = band // NI * 16 + pw // 4
    return z, pw % 4, band % NI


def device(z, y, i):
    return (z // 16 * NI + i, z % 16 * 4 + y)


def parity(z):
    return (z + 24) % NZ // 16


def fourier():
    at = np.arange(GRID)
    turn = np.float32(2.0 * math.pi / GRID) * (at[:, None] * at[None, :] % GRID).astype(np.float32)
    cos, sin = np.cos(turn), np.sin(turn)
    return np.concatenate([np.concatenate([cos, -sin], 1), np.concatenate([sin, cos], 1)], 0)


def band_choice():
    choice = np.zeros((2, NI, 2, 4, 2, 32), np.float32)
    for i in range(NI):
        for k in range(4):
            b = k // 2 * 16 + 2 * i + k % 2
            choice[0, i, 0, k, 0, b] = 1.0
            choice[0, i, 1, k, 1, b] = 1.0
            choice[1, i, 0, k, 1, b] = 1.0
            choice[1, i, 1, k, 0, b] = -1.0
    return choice.reshape(128, 64)


def plane_order():
    order = np.zeros((2, 4, 16, 128), np.float32)
    for high in range(2):
        for y in range(4):
            for low in range(16):
                k = 2 * ((low + 8) % 16 * 4 + y) + parity(high * 16 + low)
                order[high, y, low, k] = 1.0
    return order.reshape(128, 128)


def column_forms():
    expand = np.zeros((2, NI, 2, 2, 4, 2, 4, 2, NI), np.float32)
    keep = np.zeros((4, 2, 2, STICK, 4, 2, 4, 2, NI), np.float32)
    fold = np.zeros((2, STICK, 4, 2, 2, STICK), np.float32)
    for half in range(2):
        for i in range(NI):
            for octet in range(2):
                for bit in range(2):
                    expand[half, i, octet, bit, 2 * half + octet, bit, :, :, i] = 1.0
    for bits in range(4):
        for y in range(2):
            keep[bits, :, y, :, :, :, bits, y, :] = 1.0
    for y in range(2):
        for s in range(STICK):
            fold[y, s, :, y, :, s] = 1.0
    return expand.reshape(64, 512), keep.reshape(128, 512), fold.reshape(16, 128)


def dot(a, b):
    return jnp.dot(a, b, preferred_element_type=jnp.float32)


def dot_across(a, b):
    return lax.dot_general(a, b, ACROSS, preferred_element_type=jnp.float32)


def narrow(a):
    return a.astype(jnp.bfloat16)


def wide(a):
    return a.astype(jnp.float32)


def kernel(
    scale,
    coeffs,
    rotation,
    lengths,
    columns,
    planes,
    occupation,
    table,
    choice,
    order,
    expand,
    only,
    fold,
    out,
    send,
    recv,
    staged,
    sticks,
    turned,
    xs,
    ys,
    share_own,
    spread,
    hits,
    total,
    half,
    part,
    shares,
    mine,
    held,
    share_other,
    s1,
    r1,
    s2,
    r2,
    s3,
    r3,
    s4,
    r4,
    s5,
    r5,
    own,
    s6,
    r6,
):
    z, y, i = place()
    q = y * NI + i

    def near(t):
        return device(z, t // NI, t % NI)

    def far(t):
        return device(t, y, i)

    barrier = pltpu.get_barrier_semaphore()

    @pl.loop(1, NZ)
    def _(p):
        pl.semaphore_signal(barrier, inc=1, device_id=far((z + p) % NZ), device_id_type=MESH)

    @pl.loop(1, NQ)
    def _(p):
        pl.semaphore_signal(barrier, inc=1, device_id=near((q + p) % NQ), device_id_type=MESH)

    for b in range(2):
        share_own[b] = jnp.zeros((8, 128), jnp.float32) + wide(occupation[b])

    with jax.named_scope("transform"):
        real, imag = rotation[0], rotation[1]
        to_real, to_imag = choice[:, 0:32], choice[:, 32:64]
        forms = jnp.concatenate(
            [
                dot(to_real, real) + dot(to_imag, imag),
                dot(to_imag, real) - dot(to_real, imag),
            ],
            1,
        )
        forms = narrow(forms)
        by_stick = narrow(jnp.swapaxes(wide(coeffs[...]), 0, 1))
        first_row = (lax.axis_index("band") * lax.axis_size("pw") + lax.axis_index("pw")) * STICK
        at_j = lax.broadcasted_iota(jnp.int32, (1, GRID), 1)
        lane_stick = lax.broadcasted_iota(jnp.int32, (1, 128), 1) % 64 // VALS
        shift = jnp.zeros((1, 128), jnp.int32)
        for s in range(STICK):
            length = lengths[first_row + s]
            shift = jnp.where(lane_stick == s, length // 2, shift)
            live = jnp.where(at_j < length, 1.0, 0.0)
            rotated = wide(narrow(dot(forms, by_stick[s]))) * live
            for t in range(2):
                turned[:, s, :, t * GRID : (t + 1) * GRID] = rotated[
                    t * 64 : t * 64 + 64
                ].reshape(NI, VALS, GRID)
        rows = narrow(turned[...].reshape(NI * STICK * VALS, 2 * GRID))
        plane = jnp.broadcast_to(wide(planes[...]), (128, 128)).T.astype(jnp.int32)
        lane = lax.broadcasted_iota(jnp.int32, (128, 128), 1)
        picked = narrow(
            jnp.concatenate(
                [jnp.where(plane == lane, 1.0, 0.0), jnp.where(plane == lane + 128, 1.0, 0.0)], 1
            )
        )
        waves0 = narrow(dot(picked, table[0:GRID, :]))
        waves1 = narrow(dot(picked, table[GRID : 2 * GRID, :]))
        angle = wide(plane * shift % GRID) * (2.0 * math.pi / GRID)
        cos = jnp.concatenate([jnp.cos(angle)] * 4, 1)
        sin = jnp.concatenate([jnp.sin(angle)] * 4, 1)
        values = dot_across(waves0, rows) * cos + dot_across(waves1, rows) * sin
    values = dot(order[...], narrow(values))
    left = lax.broadcasted_iota(jnp.int32, (16, 128), 1) < 64
    for b in range(4):
        for pair in range(4):
            lower = values[b * 16 : b * 16 + 16, pair * 128 : pair * 128 + 128]
            upper = values[64 + b * 16 : 80 + b * 16, pair * 128 : pair * 128 + 128]
            at = b * NI + 2 * pair
            send[at] = narrow(jnp.where(left, lower, pltpu.roll(upper, 64, 1)))
            send[at + 1] = narrow(jnp.where(left, pltpu.roll(lower, 64, 1), upper))

    with jax.named_scope("columns"):
        natural = wide(columns[...]).T.astype(jnp.int32)
        for part_of, into in ((natural // GRID, xs), (natural % GRID, ys)):
            moved = dot(narrow(wide(part_of)), expand[...])
            moved = dot(fold[...], narrow(moved * wide(only[...]))).astype(jnp.int32)
            for b in range(4):
                into[b] = moved[:, b * 128 : b * 128 + 128]
        total[...] = jnp.zeros_like(total)

    with jax.named_scope("entry"):
        pl.semaphore_wait(barrier, NZ + NQ - 2)

    def first(slot_src, slot_dst, target):
        return pltpu.make_async_remote_copy(
            src_ref=send.at[slot_src],
            dst_ref=recv.at[slot_dst],
            send_sem=s1.at[slot_src],
            recv_sem=r1.at[slot_dst],
            device_id=target,
            device_id_type=MESH,
        )

    def second(slot_src, slot_dst, target):
        return pltpu.make_async_remote_copy(
            src_ref=staged.at[slot_src],
            dst_ref=sticks.at[slot_dst],
            send_sem=s2.at[slot_src],
            recv_sem=r2.at[slot_dst],
            device_id=target,
            device_id_type=MESH,
        )

    @pl.loop(1, NQ)
    def _(p):
        t = (q + p) % NQ
        first(t, q, near(t)).start()

    weights = pltpu.make_async_remote_copy(
        src_ref=share_own,
        dst_ref=share_other,
        send_sem=s6,
        recv_sem=r6,
        device_id=far((z + 16) % NZ),
        device_id_type=MESH,
    )
    weights.start()
    keep = pltpu.make_async_copy(send.at[q], recv.at[q], own.at[0])
    keep.start()
    keep.wait()

    with jax.named_scope("near"):

        @pl.loop(1, NQ)
        def _(p):
            t = (q + NQ - p) % NQ
            first(t, t, near(t)).wait_recv()

    swapped = jnp.swapaxes(wide(recv[...]), 0, 1)
    lower, upper = swapped[:, :16], swapped[:, 16:]
    left = lax.broadcasted_iota(jnp.int32, lower.shape, 2) < 64
    staged[0:16] = narrow(jnp.where(left, lower, pltpu.roll(upper, 64, 2)))
    staged[16:32] = narrow(jnp.where(left, pltpu.roll(lower, 64, 2), upper))

    @pl.loop(1, NZ)
    def _(p):
        t = (z + (16 + p // 2 * (1 - p % 2 * 2))) % NZ
        second(t, z, far(t)).start()

    keep2 = pltpu.make_async_copy(staged.at[z], sticks.at[z], own.at[1])
    keep2.start()
    keep2.wait()

    @pl.loop(0, 4)
    def _(step):
        octet = (z // 8 + step + step // 2 - 2 * (step // 3)) % 4

        with jax.named_scope("arrive"):

            @pl.loop(0, 8)
            def _(p):
                t = octet * 8 + p

                @pl.when(t != z)
                def _():
                    second(t, t, far(t)).wait_recv()

        with jax.named_scope("scatter"):
            block = wide(sticks[pl.ds(octet * 8, 8)].reshape(128, 128)).T
            value = narrow(block.reshape(16, VALS, 128))
            grid_at = lax.broadcasted_iota(jnp.int32, (GRID, 128), 0)
            for b in range(16):
                at = slice(b * 128, b * 128 + 128)
                hit = jnp.where(grid_at == xs[octet, b : b + 1, :], 1.0, 0.0)
                hits[0, :, at] = narrow(hit)
                hit = jnp.where(grid_at == ys[octet, b : b + 1, :], 1.0, 0.0)
                hits[1, :, at] = narrow(hit)
            for m in range(4):
                for v in (2 * m, 2 * m + 1):
                    for b in range(16):
                        at = slice(b * 128, b * 128 + 128)
                        spread[v * GRID : (v + 1) * GRID, at] = (
                            hits[1, :, at] * value[b, v : v + 1, :]
                        )
                at = slice(m * 512, m * 512 + 512)
                total[at, :] += dot_across(spread[at, :], hits[0])

    weights.wait_recv()
    low = z < 16
    for b in range(4):
        real = total[b * GRID : (b + 1) * GRID, :]
        imag = total[(4 + b) * GRID : (5 + b) * GRID, :]
        mid = narrow(dot(table[...], narrow(jnp.concatenate([real, imag], 0))))
        half[:, 0:GRID] = mid[0:GRID]
        half[:, GRID : 2 * GRID] = mid[GRID : 2 * GRID]
        wave = dot_across(table[...], half[...])
        power = wave[0:GRID] * wave[0:GRID] + wave[GRID:] * wave[GRID:]
        here, there = share_own[b % 2, 0:1, :], share_other[b % 2, 0:1, :]
        weight = jnp.where(low, here, there) if b < 2 else jnp.where(low, there, here)
        term = power * (jnp.concatenate([weight, weight], 1) * scale)
        dens = term if b == 0 else dens + term
    part[...] = narrow(dens.reshape(NI, HIGH, GRID))

    def share(src, dst, t):
        return pltpu.make_async_remote_copy(
            src_ref=part.at[src],
            dst_ref=shares.at[dst],
            send_sem=s3.at[src],
            recv_sem=r3.at[dst],
            device_id=device(z, y, t),
            device_id_type=MESH,
        )

    @pl.loop(1, NI)
    def _(p):
        t = (i + p) % NI
        share(t, i, t).start()

    shares[i] = part[i]

    with jax.named_scope("shares"):

        @pl.loop(1, NI)
        def _(p):
            t = (i + NI - p) % NI
            share(t, t, t).wait_recv()

    summed = wide(shares[0])
    for t in range(1, NI):
        summed = summed + wide(shares[t])
    mine[...] = narrow(summed)
    slot = parity(z)
    up, down = (z + 8) % NZ, (z + 24) % NZ

    def hop(which, at, t):
        return pltpu.make_async_remote_copy(
            src_ref=mine,
            dst_ref=held.at[at],
            send_sem=s4.at[which],
            recv_sem=r4.at[at],
            device_id=far(t),
            device_id_type=MESH,
        )

    hop(0, slot, up).start()
    hop(1, slot, down).start()

    def spread_out(k, src, t):
        return pltpu.make_async_remote_copy(
            src_ref=held.at[k],
            dst_ref=out.at[k, src],
            send_sem=s5.at[k, t],
            recv_sem=r5.at[k, src],
            device_id=device(z, y, t),
            device_id_type=MESH,
        )

    for k in range(2):
        with jax.named_scope("hop"):
            hop(0, k, up).wait_recv()

        @pl.loop(1, NI)
        def _(p):
            t = (i + p) % NI
            spread_out(k, i, t).start()

        out[k, i] = held[k]

    with jax.named_scope("gather"):
        for k in range(2):

            @pl.loop(1, NI)
            def _(p):
                t = (i + NI - p) % NI
                spread_out(k, t, t).wait_recv()

    weights.wait_send()
    hop(0, slot, up).wait_send()
    hop(1, slot, down).wait_send()

    @pl.loop(1, NI)
    def _(p):
        t = (i + p) % NI
        share(t, t, t).wait_send()
        for k in range(2):
            spread_out(k, t, t).wait_send()

    @pl.loop(1, NQ)
    def _(p):
        t = (q + p) % NQ
        first(t, t, near(t)).wait_send()

    @pl.loop(1, NZ)
    def _(p):
        t = (z + p) % NZ
        second(t, t, far(t)).wait_send()


def shards(coeffs, rotation_matrix, stick_length, stick_column, plane_index, occupation):
    band_count = lax.axis_size("band")
    scale = 1.0 / float(occupation.shape[0] * band_count * stick_column.shape[0] * GRID)
    vmem = pl.BlockSpec(memory_space=pltpu.VMEM)
    smem = pl.BlockSpec(memory_space=pltpu.SMEM)
    dma = pltpu.SemaphoreType.DMA
    bf16, f32 = jnp.bfloat16, jnp.float32
    result = pl.pallas_call(
        lambda *refs: kernel(scale, *refs),
        out_shape=jax.ShapeDtypeStruct((2, NI, HIGH, GRID), bf16),
        in_specs=[vmem, vmem, smem, vmem, vmem, smem] + [vmem] * 6,
        out_specs=vmem,
        scratch_shapes=[
            pltpu.VMEM((NQ, 16, 128), bf16),
            pltpu.VMEM((NQ, 16, 128), bf16),
            pltpu.VMEM((NZ, 16, 128), bf16),
            pltpu.VMEM((NZ, 16, 128), bf16),
            pltpu.VMEM((NI, STICK, VALS, 2 * GRID), f32),
            pltpu.VMEM((4, 16, 128), jnp.int32),
            pltpu.VMEM((4, 16, 128), jnp.int32),
            pltpu.VMEM((2, 8, 128), f32),
            pltpu.VMEM((VALS * GRID, OCTET), bf16),
            pltpu.VMEM((2, GRID, OCTET), bf16),
            pltpu.VMEM((VALS * GRID, GRID), f32),
            pltpu.VMEM((GRID, 2 * GRID), bf16),
            pltpu.VMEM((NI, HIGH, GRID), bf16),
            pltpu.VMEM((NI, HIGH, GRID), bf16),
            pltpu.VMEM((HIGH, GRID), bf16),
            pltpu.VMEM((2, HIGH, GRID), bf16),
            pltpu.VMEM((2, 8, 128), f32),
            dma((NQ,)),
            dma((NQ,)),
            dma((NZ,)),
            dma((NZ,)),
            dma((NI,)),
            dma((NI,)),
            dma((2,)),
            dma((2,)),
            dma((2, NI)),
            dma((2, NI)),
            dma((2,)),
            dma,
            dma,
        ],
        compiler_params=pltpu.CompilerParams(
            collective_id=1, has_side_effects=True, vmem_limit_bytes=VMEM_LIMIT
        ),
        name="density",
    )(
        coeffs.reshape(128, STICK, GRID),
        jnp.transpose(rotation_matrix, (0, 2, 1)),
        stick_length,
        stick_column.reshape(64, 128),
        plane_index.reshape(1, 128),
        occupation,
        *(jnp.asarray(form, bf16) for form in (fourier(), band_choice(), plane_order())),
        *(jnp.asarray(form, bf16) for form in column_forms()),
    )
    return wide(result.reshape(2, GRID, GRID))


def solution(mesh):
    return jax.shard_map(
        shards,
        mesh=mesh,
        in_specs=(P(None, None, ("band", "pw"), None), P(), P(), P(), P(), P("band")),
        out_specs=P("pw", None, None),
        check_vma=False,
    )
```

```python
import math

import jax
import jax.numpy as jnp
import numpy as np
from jax import lax
from jax.experimental import pallas as pl
from jax.experimental.pallas import tpu as pltpu
from jax.sharding import PartitionSpec as P

MESH = pl.DeviceIdType.MESH
GRID = 256
NZ = 32
NI = 8
NQ = 32
STICK = 8
VALS = 8
OCTET = 8 * 16 * 16
HIGH = GRID // NI
VMEM_LIMIT = 62 * 1024 * 1024
ACROSS = (((1,), (1,)), ((), ()))


def place():
    band = lax.axis_index("band")
    pw = lax.axis_index("pw")
    z = band // NI * 16 + pw // 4
    return z, pw % 4, band % NI


def device(z, y, i):
    return (z // 16 * NI + i, z % 16 * 4 + y)


def parity(z):
    return (z + 24) % NZ // 16


def fourier():
    at = np.arange(GRID)
    turn = np.float32(2.0 * math.pi / GRID) * (at[:, None] * at[None, :] % GRID).astype(np.float32)
    cos, sin = np.cos(turn), np.sin(turn)
    return np.concatenate([np.concatenate([cos, -sin], 1), np.concatenate([sin, cos], 1)], 0)


def band_choice():
    choice = np.zeros((2, NI, 2, 4, 2, 32), np.float32)
    for i in range(NI):
        for k in range(4):
            b = k // 2 * 16 + 2 * i + k % 2
            choice[0, i, 0, k, 0, b] = 1.0
            choice[0, i, 1, k, 1, b] = 1.0
            choice[1, i, 0, k, 1, b] = 1.0
            choice[1, i, 1, k, 0, b] = -1.0
    return choice.reshape(128, 64)


def plane_order():
    order = np.zeros((2, 4, 16, 128), np.float32)
    for high in range(2):
        for y in range(4):
            for low in range(16):
                k = 2 * ((low + 8) % 16 * 4 + y) + parity(high * 16 + low)
                order[high, y, low, k] = 1.0
    return order.reshape(128, 128)


def column_forms():
    expand = np.zeros((2, NI, 2, 2, 4, 2, 4, 2, NI), np.float32)
    keep = np.zeros((4, 2, 2, STICK, 4, 2, 4, 2, NI), np.float32)
    fold = np.zeros((2, STICK, 4, 2, 2, STICK), np.float32)
    for half in range(2):
        for i in range(NI):
            for octet in range(2):
                for bit in range(2):
                    expand[half, i, octet, bit, 2 * half + octet, bit, :, :, i] = 1.0
    for bits in range(4):
        for y in range(2):
            keep[bits, :, y, :, :, :, bits, y, :] = 1.0
    for y in range(2):
        for s in range(STICK):
            fold[y, s, :, y, :, s] = 1.0
    return expand.reshape(64, 512), keep.reshape(128, 512), fold.reshape(16, 128)


def dot(a, b):
    return jnp.dot(a, b, preferred_element_type=jnp.float32)


def dot_across(a, b):
    return lax.dot_general(a, b, ACROSS, preferred_element_type=jnp.float32)


def narrow(a):
    return a.astype(jnp.bfloat16)


def wide(a):
    return a.astype(jnp.float32)


def kernel(
    scale,
    *refs,
):
    given, out, fetched, rest = refs[:12], refs[12], refs[13:25], refs[25:]
    (coeffs, rotation, lengths, columns, planes, occupation, table, choice, order, expand, only, fold) = fetched
    (send, recv, staged, sticks, turned, xs, ys, share_own, spread, hit_x, hit_y, total, half, part, shares, mine, held, share_other, s1, r1, s2, r2, s3, r3, s4, r4, s5, r5, own, s6, r6, fetch, word) = rest
    z, y, i = place()
    q = y * NI + i

    def near(t):
        return device(z, t // NI, t % NI)

    def far(t):
        return device(t, y, i)

    barrier = pltpu.get_barrier_semaphore()

    @pl.loop(1, NQ)
    def _(p):
        pl.semaphore_signal(barrier, inc=1, device_id=near((q + p) % NQ), device_id_type=MESH)

    @pl.loop(1, 5)
    def _(p):
        for t in ((z + p) % NZ, (z + NZ - p) % NZ):
            pl.semaphore_signal(barrier, inc=1, device_id=far(t), device_id_type=MESH)

    def tell(n, distance):
        for t in ((z + distance) % NZ, (z + NZ - distance) % NZ):
            pl.semaphore_signal(word.at[n], inc=1, device_id=far(t), device_id_type=MESH)

    def hear(n):
        pl.semaphore_wait(word.at[n], 2)

    fetches = [
        pltpu.make_async_copy(source, target, fetch.at[n])
        for n, (source, target) in enumerate(zip(given, fetched))
    ]
    for copy in fetches:
        copy.start()
    for copy in fetches:
        copy.wait()
    for b in range(2):
        share_own[b] = jnp.zeros((8, 128), jnp.float32) + wide(occupation[b])

    with jax.named_scope("transform"):
        real, imag = rotation[0], rotation[1]
        to_real, to_imag = choice[:, 0:32], choice[:, 32:64]
        forms = jnp.concatenate(
            [
                dot(to_real, real) + dot(to_imag, imag),
                dot(to_imag, real) - dot(to_real, imag),
            ],
            1,
        )
        forms = narrow(forms)
        by_stick = narrow(jnp.swapaxes(wide(coeffs[...]), 0, 1))
        first_row = (lax.axis_index("band") * lax.axis_size("pw") + lax.axis_index("pw")) * STICK
        at_j = lax.broadcasted_iota(jnp.int32, (1, GRID), 1)
        lane_stick = lax.broadcasted_iota(jnp.int32, (1, 128), 1) % 64 // VALS
        shift = jnp.zeros((1, 128), jnp.int32)
        for s in range(STICK):
            length = lengths[first_row + s]
            shift = jnp.where(lane_stick == s, length // 2, shift)
            live = jnp.where(at_j < length, 1.0, 0.0)
            rotated = wide(narrow(dot(forms, by_stick[s]))) * live
            for t in range(2):
                turned[:, s, :, t * GRID : (t + 1) * GRID] = rotated[
                    t * 64 : t * 64 + 64
                ].reshape(NI, VALS, GRID)
        rows = narrow(turned[...].reshape(NI * STICK * VALS, 2 * GRID))
        pl.semaphore_wait(barrier, NQ + 7)
        tell(0, 4)
        plane = jnp.broadcast_to(wide(planes[...]), (128, 128)).T.astype(jnp.int32)
        lane = lax.broadcasted_iota(jnp.int32, (128, 128), 1)
        picked = narrow(
            jnp.concatenate(
                [jnp.where(plane == lane, 1.0, 0.0), jnp.where(plane == lane + 128, 1.0, 0.0)], 1
            )
        )
        waves0 = narrow(dot(picked, table[0:GRID, :]))
        waves1 = narrow(dot(picked, table[GRID : 2 * GRID, :]))
        angle = wide(plane * shift % GRID) * (2.0 * math.pi / GRID)
        cos = jnp.concatenate([jnp.cos(angle)] * 4, 1)
        sin = jnp.concatenate([jnp.sin(angle)] * 4, 1)
        values = dot_across(waves0, rows) * cos + dot_across(waves1, rows) * sin
    values = dot(order[...], narrow(values))
    left = lax.broadcasted_iota(jnp.int32, (16, 128), 1) < 64
    for b in range(4):
        for pair in range(4):
            lower = values[b * 16 : b * 16 + 16, pair * 128 : pair * 128 + 128]
            upper = values[64 + b * 16 : 80 + b * 16, pair * 128 : pair * 128 + 128]
            at = b * NI + 2 * pair
            send[at] = narrow(jnp.where(left, lower, pltpu.roll(upper, 64, 1)))
            send[at + 1] = narrow(jnp.where(left, pltpu.roll(lower, 64, 1), upper))

    def first(slot_src, slot_dst, target):
        return pltpu.make_async_remote_copy(
            src_ref=send.at[slot_src],
            dst_ref=recv.at[slot_dst],
            send_sem=s1.at[slot_src],
            recv_sem=r1.at[slot_dst],
            device_id=target,
            device_id_type=MESH,
        )

    def second(slot_src, slot_dst, target):
        return pltpu.make_async_remote_copy(
            src_ref=staged.at[slot_src],
            dst_ref=sticks.at[slot_dst],
            send_sem=s2.at[slot_src],
            recv_sem=r2.at[slot_dst],
            device_id=target,
            device_id_type=MESH,
        )

    @pl.loop(1, NQ)
    def _(p):
        t = (q + p) % NQ
        first(t, q, near(t)).start()

    hear(0)
    tell(1, 8)
    with jax.named_scope("columns"):
        natural = wide(columns[...]).T.astype(jnp.int32)
        into = []
        for part_of in (natural // GRID, natural % GRID):
            moved = dot(narrow(wide(part_of)), expand[...])
            moved = dot(fold[...], narrow(moved * wide(only[...])))
            into.append(moved)
        for n in range(4):
            part_of = jnp.concatenate([into[0][:, n * 128 : n * 128 + 128]] * 8, 0).T
            xs[n] = part_of.astype(jnp.int32)
            ys[n] = into[1][:, n * 128 : n * 128 + 128].astype(jnp.int32)
        total[...] = jnp.zeros_like(total)

    weights = pltpu.make_async_remote_copy(
        src_ref=share_own,
        dst_ref=share_other,
        send_sem=s6,
        recv_sem=r6,
        device_id=far((z + 16) % NZ),
        device_id_type=MESH,
    )
    keep = pltpu.make_async_copy(send.at[q], recv.at[q], own.at[0])
    keep.start()
    keep.wait()

    with jax.named_scope("near"):

        @pl.loop(1, NQ)
        def _(p):
            t = (q + NQ - p) % NQ
            first(t, t, near(t)).wait_recv()

    swapped = jnp.swapaxes(wide(recv[...]), 0, 1)
    lower, upper = swapped[:, :16], swapped[:, 16:]
    left = lax.broadcasted_iota(jnp.int32, lower.shape, 2) < 64
    staged[0:16] = narrow(jnp.where(left, lower, pltpu.roll(upper, 64, 2)))
    staged[16:32] = narrow(jnp.where(left, pltpu.roll(lower, 64, 2), upper))

    hear(1)
    weights.start()

    @pl.loop(1, 7)
    def _(p):
        away = (p + 1) // 2
        t = (z + p % 2 * away + (1 - p % 2) * (NZ - away)) % NZ
        second(t, z, far(t)).start()

    @pl.loop(1, NZ - 6)
    def _(p):
        t = (z + (16 + p // 2 * (1 - p % 2 * 2))) % NZ
        second(t, z, far(t)).start()

    keep2 = pltpu.make_async_copy(staged.at[z], sticks.at[z], own.at[1])
    keep2.start()
    keep2.wait()

    with jax.named_scope("where"):

        @pl.loop(0, 4)
        def _(n):
            down = lax.broadcasted_iota(jnp.int32, (GRID, 128), 0)
            right = lax.broadcasted_iota(jnp.int32, (128, GRID), 1)
            for b in range(16):
                at = slice(b * 128, b * 128 + 128)
                hit = jnp.where(right == xs[n, :, b : b + 1], 1.0, 0.0)
                hit_x[n, at, :] = narrow(hit)
                hit = jnp.where(down == ys[n, b : b + 1, :], 1.0, 0.0)
                hit_y[n, :, at] = narrow(hit)

    @pl.loop(0, 4)
    def _(step):
        octet = (z // 8 + step * 2 % 3 + step // 3 * 3) % 4

        with jax.named_scope("arrive"):

            @pl.loop(0, 8)
            def _(p):
                t = octet * 8 + p

                @pl.when(t != z)
                def _():
                    second(t, t, far(t)).wait_recv()

        with jax.named_scope("scatter"):
            block = wide(sticks[pl.ds(octet * 8, 8)].reshape(128, 128)).T
            value = narrow(block.reshape(16, VALS, 128))
            for m in range(4):
                for v in (2 * m, 2 * m + 1):
                    for b in range(16):
                        at = slice(b * 128, b * 128 + 128)
                        spread[v * GRID : (v + 1) * GRID, at] = (
                            hit_y[octet, :, at] * value[b, v : v + 1, :]
                        )
                at = slice(m * 512, m * 512 + 512)
                total[at, :] += dot(spread[at, :], hit_x[octet])

    weights.wait_recv()
    low = z < 16
    for b in range(4):
        real = total[b * GRID : (b + 1) * GRID, :]
        imag = total[(4 + b) * GRID : (5 + b) * GRID, :]
        mid = narrow(dot(table[...], narrow(jnp.concatenate([real, imag], 0))))
        half[:, 0:GRID] = mid[0:GRID]
        half[:, GRID : 2 * GRID] = mid[GRID : 2 * GRID]
        wave = dot_across(table[...], half[...])
        power = wave[0:GRID] * wave[0:GRID] + wave[GRID:] * wave[GRID:]
        here, there = share_own[b % 2, 0:1, :], share_other[b % 2, 0:1, :]
        weight = jnp.where(low, here, there) if b < 2 else jnp.where(low, there, here)
        term = power * (jnp.concatenate([weight, weight], 1) * scale)
        dens = term if b == 0 else dens + term
    part[...] = narrow(dens.reshape(NI, HIGH, GRID))

    def share(src, dst, t):
        return pltpu.make_async_remote_copy(
            src_ref=part.at[src],
            dst_ref=shares.at[dst],
            send_sem=s3.at[src],
            recv_sem=r3.at[dst],
            device_id=device(z, y, t),
            device_id_type=MESH,
        )

    @pl.loop(1, NI)
    def _(p):
        t = (i + p) % NI
        share(t, i, t).start()

    shares[i] = part[i]

    with jax.named_scope("shares"):

        @pl.loop(1, NI)
        def _(p):
            t = (i + NI - p) % NI
            share(t, t, t).wait_recv()

    summed = wide(shares[0])
    for t in range(1, NI):
        summed = summed + wide(shares[t])
    mine[...] = narrow(summed)
    slot = parity(z)
    up, down = (z + 8) % NZ, (z + 24) % NZ

    def hop(which, at, t):
        return pltpu.make_async_remote_copy(
            src_ref=mine,
            dst_ref=held.at[at],
            send_sem=s4.at[which],
            recv_sem=r4.at[at],
            device_id=far(t),
            device_id_type=MESH,
        )

    hop(0, slot, up).start()
    hop(1, slot, down).start()

    def spread_out(k, src, t):
        return pltpu.make_async_remote_copy(
            src_ref=held.at[k],
            dst_ref=out.at[k, src],
            send_sem=s5.at[k, t],
            recv_sem=r5.at[k, src],
            device_id=device(z, y, t),
            device_id_type=MESH,
        )

    for k in range(2):
        with jax.named_scope("hop"):
            hop(0, k, up).wait_recv()

        @pl.loop(1, NI)
        def _(p):
            t = (i + p) % NI
            spread_out(k, i, t).start()

        out[k, i] = held[k]

    with jax.named_scope("gather"):
        for k in range(2):

            @pl.loop(1, NI)
            def _(p):
                t = (i + NI - p) % NI
                spread_out(k, t, t).wait_recv()

    weights.wait_send()
    hop(0, slot, up).wait_send()
    hop(1, slot, down).wait_send()

    @pl.loop(1, NI)
    def _(p):
        t = (i + p) % NI
        share(t, t, t).wait_send()
        for k in range(2):
            spread_out(k, t, t).wait_send()

    @pl.loop(1, NQ)
    def _(p):
        t = (q + p) % NQ
        first(t, t, near(t)).wait_send()

    @pl.loop(1, NZ)
    def _(p):
        t = (z + p) % NZ
        second(t, t, far(t)).wait_send()


def shards(coeffs, rotation_matrix, stick_length, stick_column, plane_index, occupation):
    band_count = lax.axis_size("band")
    scale = 1.0 / float(occupation.shape[0] * band_count * stick_column.shape[0] * GRID)
    bf16, f32 = jnp.bfloat16, jnp.float32
    vmem = pl.BlockSpec(memory_space=pltpu.VMEM)
    given = (
        coeffs.reshape(128, STICK, GRID),
        jnp.transpose(rotation_matrix, (0, 2, 1)),
        stick_length,
        stick_column.reshape(64, 128),
        plane_index.reshape(1, 128),
        occupation,
        *(jnp.asarray(form, bf16) for form in (fourier(), band_choice(), plane_order())),
        *(jnp.asarray(form, bf16) for form in column_forms()),
    )
    dma = pltpu.SemaphoreType.DMA
    result = pl.pallas_call(
        lambda *refs: kernel(scale, *refs),
        out_shape=jax.ShapeDtypeStruct((2, NI, HIGH, GRID), bf16),
        in_specs=[pl.BlockSpec(memory_space=pl.ANY)] * len(given),
        out_specs=vmem,
        scratch_shapes=[
            *(
                (pltpu.SMEM if n in (2, 5) else pltpu.VMEM)(form.shape, form.dtype)
                for n, form in enumerate(given)
            ),
            pltpu.VMEM((NQ, 16, 128), bf16),
            pltpu.VMEM((NQ, 16, 128), bf16),
            pltpu.VMEM((NZ, 16, 128), bf16),
            pltpu.VMEM((NZ, 16, 128), bf16),
            pltpu.VMEM((NI, STICK, VALS, 2 * GRID), f32),
            pltpu.VMEM((4, 128, 128), jnp.int32),
            pltpu.VMEM((4, 16, 128), jnp.int32),
            pltpu.VMEM((2, 8, 128), f32),
            pltpu.VMEM((VALS * GRID, OCTET), bf16),
            pltpu.VMEM((4, OCTET, GRID), bf16),
            pltpu.VMEM((4, GRID, OCTET), bf16),
            pltpu.VMEM((VALS * GRID, GRID), f32),
            pltpu.VMEM((GRID, 2 * GRID), bf16),
            pltpu.VMEM((NI, HIGH, GRID), bf16),
            pltpu.VMEM((NI, HIGH, GRID), bf16),
            pltpu.VMEM((HIGH, GRID), bf16),
            pltpu.VMEM((2, HIGH, GRID), bf16),
            pltpu.VMEM((2, 8, 128), f32),
            dma((NQ,)),
            dma((NQ,)),
            dma((NZ,)),
            dma((NZ,)),
            dma((NI,)),
            dma((NI,)),
            dma((2,)),
            dma((2,)),
            dma((2, NI)),
            dma((2, NI)),
            dma((2,)),
            dma,
            dma,
            dma((len(given),)),
            pltpu.SemaphoreType.REGULAR((2,)),
        ],
        compiler_params=pltpu.CompilerParams(
            collective_id=1, has_side_effects=True, vmem_limit_bytes=VMEM_LIMIT
        ),
        name="density",
    )(*given)
    return wide(result.reshape(2, GRID, GRID))


def solution(mesh):
    return jax.shard_map(
        shards,
        mesh=mesh,
        in_specs=(P(None, None, ("band", "pw"), None), P(), P(), P(), P(), P("band")),
        out_specs=P("pw", None, None),
        check_vma=False,
    )
```

```python
import math

import jax
import jax.numpy as jnp
import numpy as np
from jax import lax
from jax.experimental import pallas as pl
from jax.experimental.pallas import tpu as pltpu
from jax.sharding import PartitionSpec as P

MESH = pl.DeviceIdType.MESH
GRID = 256
NZ = 32
NI = 8
NQ = 32
STICK = 8
VALS = 8
OCTET = 8 * 16 * 16
HIGH = GRID // NI
VMEM_LIMIT = 62 * 1024 * 1024
ACROSS = (((1,), (1,)), ((), ()))


def place():
    band = lax.axis_index("band")
    pw = lax.axis_index("pw")
    z = band // NI * 16 + pw // 4
    return z, pw % 4, band % NI


def device(z, y, i):
    return (z // 16 * NI + i, z % 16 * 4 + y)


def parity(z):
    return (z + 24) % NZ // 16


def fourier():
    at = np.arange(GRID)
    turn = np.float32(2.0 * math.pi / GRID) * (at[:, None] * at[None, :] % GRID).astype(np.float32)
    cos, sin = np.cos(turn), np.sin(turn)
    return np.concatenate([np.concatenate([cos, -sin], 1), np.concatenate([sin, cos], 1)], 0)


def band_choice():
    choice = np.zeros((2, NI, 2, 4, 2, 32), np.float32)
    for i in range(NI):
        for k in range(4):
            b = k // 2 * 16 + 2 * i + k % 2
            choice[0, i, 0, k, 0, b] = 1.0
            choice[0, i, 1, k, 1, b] = 1.0
            choice[1, i, 0, k, 1, b] = 1.0
            choice[1, i, 1, k, 0, b] = -1.0
    return choice.reshape(128, 64)


def plane_order():
    order = np.zeros((2, 4, 16, 128), np.float32)
    for high in range(2):
        for y in range(4):
            for low in range(16):
                k = 2 * ((low + 8) % 16 * 4 + y) + parity(high * 16 + low)
                order[high, y, low, k] = 1.0
    return order.reshape(128, 128)


def column_forms():
    expand = np.zeros((2, NI, 2, 2, 4, 2, 4, 2, NI), np.float32)
    keep = np.zeros((4, 2, 2, STICK, 4, 2, 4, 2, NI), np.float32)
    fold = np.zeros((2, STICK, 4, 2, 2, STICK), np.float32)
    for half in range(2):
        for i in range(NI):
            for octet in range(2):
                for bit in range(2):
                    expand[half, i, octet, bit, 2 * half + octet, bit, :, :, i] = 1.0
    for bits in range(4):
        for y in range(2):
            keep[bits, :, y, :, :, :, bits, y, :] = 1.0
    for y in range(2):
        for s in range(STICK):
            fold[y, s, :, y, :, s] = 1.0
    return expand.reshape(64, 512), keep.reshape(128, 512), fold.reshape(16, 128)


def dot(a, b):
    return jnp.dot(a, b, preferred_element_type=jnp.float32)


def dot_across(a, b):
    return lax.dot_general(a, b, ACROSS, preferred_element_type=jnp.float32)


def narrow(a):
    return a.astype(jnp.bfloat16)


def wide(a):
    return a.astype(jnp.float32)


def kernel(
    scale,
    *refs,
):
    given, out, fetched, rest = refs[:12], refs[12], refs[13:25], refs[25:]
    (coeffs, rotation, lengths, columns, planes, occupation, table, choice, order, expand, only, fold) = fetched
    (send, recv, staged, sticks, turned, xs, ys, share_own, spread, hit_x, hit_y, total, half, part, shares, mine, held, share_other, s1, r1, s2, r2, s3, r3, s4, r4, s5, r5, own, s6, r6, fetch, word) = rest
    z, y, i = place()
    q = y * NI + i

    def near(t):
        return device(z, t // NI, t % NI)

    def far(t):
        return device(t, y, i)

    barrier = pltpu.get_barrier_semaphore()

    @pl.loop(1, NQ)
    def _(p):
        pl.semaphore_signal(barrier, inc=1, device_id=near((q + p) % NQ), device_id_type=MESH)

    @pl.loop(1, 5)
    def _(p):
        for t in ((z + p) % NZ, (z + NZ - p) % NZ):
            pl.semaphore_signal(barrier, inc=1, device_id=far(t), device_id_type=MESH)

    def tell(n, distance):
        for t in ((z + distance) % NZ, (z + NZ - distance) % NZ):
            pl.semaphore_signal(word.at[n], inc=1, device_id=far(t), device_id_type=MESH)

    def hear(n):
        pl.semaphore_wait(word.at[n], 2)

    fetches = [
        pltpu.make_async_copy(source, target, fetch.at[n])
        for n, (source, target) in enumerate(zip(given, fetched))
    ]
    for copy in fetches:
        copy.start()
    for copy in fetches:
        copy.wait()
    for b in range(2):
        share_own[b] = jnp.zeros((8, 128), jnp.float32) + wide(occupation[b])

    with jax.named_scope("transform"):
        real, imag = rotation[0], rotation[1]
        to_real, to_imag = choice[:, 0:32], choice[:, 32:64]
        forms = jnp.concatenate(
            [
                dot(to_real, real) + dot(to_imag, imag),
                dot(to_imag, real) - dot(to_real, imag),
            ],
            1,
        )
        forms = narrow(forms)
        by_stick = narrow(jnp.swapaxes(wide(coeffs[...]), 0, 1))
        first_row = (lax.axis_index("band") * lax.axis_size("pw") + lax.axis_index("pw")) * STICK
        at_j = lax.broadcasted_iota(jnp.int32, (1, GRID), 1)
        lane_stick = lax.broadcasted_iota(jnp.int32, (1, 128), 1) % 64 // VALS
        shift = jnp.zeros((1, 128), jnp.int32)
        for s in range(STICK):
            length = lengths[first_row + s]
            shift = jnp.where(lane_stick == s, length // 2, shift)
            live = jnp.where(at_j < length, 1.0, 0.0)
            rotated = wide(narrow(dot(forms, by_stick[s]))) * live
            for t in range(2):
                turned[:, s, :, t * GRID : (t + 1) * GRID] = rotated[
                    t * 64 : t * 64 + 64
                ].reshape(NI, VALS, GRID)
        rows = narrow(turned[...].reshape(NI * STICK * VALS, 2 * GRID))
        pl.semaphore_wait(barrier, NQ + 7)
        tell(0, 4)
        plane = jnp.broadcast_to(wide(planes[...]), (128, 128)).T.astype(jnp.int32)
        lane = lax.broadcasted_iota(jnp.int32, (128, 128), 1)
        picked = narrow(
            jnp.concatenate(
                [jnp.where(plane == lane, 1.0, 0.0), jnp.where(plane == lane + 128, 1.0, 0.0)], 1
            )
        )
        waves0 = narrow(dot(picked, table[0:GRID, :]))
        waves1 = narrow(dot(picked, table[GRID : 2 * GRID, :]))
        angle = wide(plane * shift % GRID) * (2.0 * math.pi / GRID)
        cos = jnp.concatenate([jnp.cos(angle)] * 4, 1)
        sin = jnp.concatenate([jnp.sin(angle)] * 4, 1)
        values = dot_across(waves0, rows) * cos + dot_across(waves1, rows) * sin
    values = dot(order[...], narrow(values))
    left = lax.broadcasted_iota(jnp.int32, (16, 128), 1) < 64
    for b in range(4):
        for pair in range(4):
            lower = values[b * 16 : b * 16 + 16, pair * 128 : pair * 128 + 128]
            upper = values[64 + b * 16 : 80 + b * 16, pair * 128 : pair * 128 + 128]
            at = b * NI + 2 * pair
            send[at] = narrow(jnp.where(left, lower, pltpu.roll(upper, 64, 1)))
            send[at + 1] = narrow(jnp.where(left, pltpu.roll(lower, 64, 1), upper))

    def first(slot_src, slot_dst, target):
        return pltpu.make_async_remote_copy(
            src_ref=send.at[slot_src],
            dst_ref=recv.at[slot_dst],
            send_sem=s1.at[slot_src],
            recv_sem=r1.at[slot_dst],
            device_id=target,
            device_id_type=MESH,
        )

    def second(slot_src, slot_dst, target):
        return pltpu.make_async_remote_copy(
            src_ref=staged.at[slot_src],
            dst_ref=sticks.at[slot_dst],
            send_sem=s2.at[slot_src],
            recv_sem=r2.at[slot_dst],
            device_id=target,
            device_id_type=MESH,
        )

    @pl.loop(1, NQ)
    def _(p):
        t = (q + p) % NQ
        first(t, q, near(t)).start()

    hear(0)
    tell(1, 8)
    with jax.named_scope("columns"):
        natural = wide(columns[...]).T.astype(jnp.int32)
        into = []
        for part_of in (natural // GRID, natural % GRID):
            moved = dot(narrow(wide(part_of)), expand[...])
            moved = dot(fold[...], narrow(moved * wide(only[...])))
            into.append(moved)
        for n in range(4):
            part_of = jnp.concatenate([into[0][:, n * 128 : n * 128 + 128]] * 8, 0).T
            xs[n] = part_of.astype(jnp.int32)
            ys[n] = into[1][:, n * 128 : n * 128 + 128].astype(jnp.int32)
        total[...] = jnp.zeros_like(total)

    weights = pltpu.make_async_remote_copy(
        src_ref=share_own,
        dst_ref=share_other,
        send_sem=s6,
        recv_sem=r6,
        device_id=far((z + 16) % NZ),
        device_id_type=MESH,
    )
    keep = pltpu.make_async_copy(send.at[q], recv.at[q], own.at[0])
    keep.start()
    keep.wait()

    with jax.named_scope("near"):

        @pl.loop(1, NQ)
        def _(p):
            t = (q + NQ - p) % NQ
            first(t, t, near(t)).wait_recv()

    swapped = jnp.swapaxes(wide(recv[...]), 0, 1)
    lower, upper = swapped[:, :16], swapped[:, 16:]
    left = lax.broadcasted_iota(jnp.int32, lower.shape, 2) < 64
    staged[0:16] = narrow(jnp.where(left, lower, pltpu.roll(upper, 64, 2)))
    staged[16:32] = narrow(jnp.where(left, pltpu.roll(lower, 64, 2), upper))

    hear(1)
    weights.start()

    @pl.loop(1, NZ)
    def _(p):
        away = (p + 1) // 2
        t = (z + p % 2 * away + (1 - p % 2) * (NZ - away)) % NZ
        second(t, z, far(t)).start()

    keep2 = pltpu.make_async_copy(staged.at[z], sticks.at[z], own.at[1])
    keep2.start()
    keep2.wait()

    with jax.named_scope("where"):

        @pl.loop(0, 4)
        def _(n):
            down = lax.broadcasted_iota(jnp.int32, (GRID, 128), 0)
            right = lax.broadcasted_iota(jnp.int32, (128, GRID), 1)
            for b in range(16):
                at = slice(b * 128, b * 128 + 128)
                hit = jnp.where(right == xs[n, :, b : b + 1], 1.0, 0.0)
                hit_x[n, at, :] = narrow(hit)
                hit = jnp.where(down == ys[n, b : b + 1, :], 1.0, 0.0)
                hit_y[n, :, at] = narrow(hit)

    @pl.loop(0, 4)
    def _(step):
        octet = (z // 8 + step + step // 2 - 2 * (step // 3)) % 4

        with jax.named_scope("arrive"):

            @pl.loop(0, 8)
            def _(p):
                t = octet * 8 + p

                @pl.when(t != z)
                def _():
                    second(t, t, far(t)).wait_recv()

        with jax.named_scope("scatter"):
            block = wide(sticks[pl.ds(octet * 8, 8)].reshape(128, 128)).T
            value = narrow(block.reshape(16, VALS, 128))
            for m in range(4):
                for v in (2 * m, 2 * m + 1):
                    for b in range(16):
                        at = slice(b * 128, b * 128 + 128)
                        spread[v * GRID : (v + 1) * GRID, at] = (
                            hit_y[octet, :, at] * value[b, v : v + 1, :]
                        )
                at = slice(m * 512, m * 512 + 512)
                total[at, :] += dot(spread[at, :], hit_x[octet])

    weights.wait_recv()
    low = z < 16
    for b in range(4):
        real = total[b * GRID : (b + 1) * GRID, :]
        imag = total[(4 + b) * GRID : (5 + b) * GRID, :]
        mid = narrow(dot(table[...], narrow(jnp.concatenate([real, imag], 0))))
        half[:, 0:GRID] = mid[0:GRID]
        half[:, GRID : 2 * GRID] = mid[GRID : 2 * GRID]
        wave = dot_across(table[...], half[...])
        power = wave[0:GRID] * wave[0:GRID] + wave[GRID:] * wave[GRID:]
        here, there = share_own[b % 2, 0:1, :], share_other[b % 2, 0:1, :]
        weight = jnp.where(low, here, there) if b < 2 else jnp.where(low, there, here)
        term = power * (jnp.concatenate([weight, weight], 1) * scale)
        dens = term if b == 0 else dens + term
    part[...] = narrow(dens.reshape(NI, HIGH, GRID))

    def share(src, dst, t):
        return pltpu.make_async_remote_copy(
            src_ref=part.at[src],
            dst_ref=shares.at[dst],
            send_sem=s3.at[src],
            recv_sem=r3.at[dst],
            device_id=device(z, y, t),
            device_id_type=MESH,
        )

    @pl.loop(1, NI)
    def _(p):
        t = (i + p) % NI
        share(t, i, t).start()

    shares[i] = part[i]

    with jax.named_scope("shares"):

        @pl.loop(1, NI)
        def _(p):
            t = (i + NI - p) % NI
            share(t, t, t).wait_recv()

    summed = wide(shares[0])
    for t in range(1, NI):
        summed = summed + wide(shares[t])
    mine[...] = narrow(summed)
    slot = parity(z)
    up, down = (z + 8) % NZ, (z + 24) % NZ

    def hop(which, at, t):
        return pltpu.make_async_remote_copy(
            src_ref=mine,
            dst_ref=held.at[at],
            send_sem=s4.at[which],
            recv_sem=r4.at[at],
            device_id=far(t),
            device_id_type=MESH,
        )

    hop(0, slot, up).start()
    hop(1, slot, down).start()

    def spread_out(k, src, t):
        return pltpu.make_async_remote_copy(
            src_ref=held.at[k],
            dst_ref=out.at[k, src],
            send_sem=s5.at[k, t],
            recv_sem=r5.at[k, src],
            device_id=device(z, y, t),
            device_id_type=MESH,
        )

    for k in range(2):
        with jax.named_scope("hop"):
            hop(0, k, up).wait_recv()

        @pl.loop(1, NI)
        def _(p):
            t = (i + p) % NI
            spread_out(k, i, t).start()

        out[k, i] = held[k]

    with jax.named_scope("gather"):
        for k in range(2):

            @pl.loop(1, NI)
            def _(p):
                t = (i + NI - p) % NI
                spread_out(k, t, t).wait_recv()

    weights.wait_send()
    hop(0, slot, up).wait_send()
    hop(1, slot, down).wait_send()

    @pl.loop(1, NI)
    def _(p):
        t = (i + p) % NI
        share(t, t, t).wait_send()
        for k in range(2):
            spread_out(k, t, t).wait_send()

    @pl.loop(1, NQ)
    def _(p):
        t = (q + p) % NQ
        first(t, t, near(t)).wait_send()

    @pl.loop(1, NZ)
    def _(p):
        t = (z + p) % NZ
        second(t, t, far(t)).wait_send()


def shards(coeffs, rotation_matrix, stick_length, stick_column, plane_index, occupation):
    band_count = lax.axis_size("band")
    scale = 1.0 / float(occupation.shape[0] * band_count * stick_column.shape[0] * GRID)
    bf16, f32 = jnp.bfloat16, jnp.float32
    vmem = pl.BlockSpec(memory_space=pltpu.VMEM)
    given = (
        coeffs.reshape(128, STICK, GRID),
        jnp.transpose(rotation_matrix, (0, 2, 1)),
        stick_length,
        stick_column.reshape(64, 128),
        plane_index.reshape(1, 128),
        occupation,
        *(jnp.asarray(form, bf16) for form in (fourier(), band_choice(), plane_order())),
        *(jnp.asarray(form, bf16) for form in column_forms()),
    )
    dma = pltpu.SemaphoreType.DMA
    result = pl.pallas_call(
        lambda *refs: kernel(scale, *refs),
        out_shape=jax.ShapeDtypeStruct((2, NI, HIGH, GRID), bf16),
        in_specs=[pl.BlockSpec(memory_space=pl.ANY)] * len(given),
        out_specs=vmem,
        scratch_shapes=[
            *(
                (pltpu.SMEM if n in (2, 5) else pltpu.VMEM)(form.shape, form.dtype)
                for n, form in enumerate(given)
            ),
            pltpu.VMEM((NQ, 16, 128), bf16),
            pltpu.VMEM((NQ, 16, 128), bf16),
            pltpu.VMEM((NZ, 16, 128), bf16),
            pltpu.VMEM((NZ, 16, 128), bf16),
            pltpu.VMEM((NI, STICK, VALS, 2 * GRID), f32),
            pltpu.VMEM((4, 128, 128), jnp.int32),
            pltpu.VMEM((4, 16, 128), jnp.int32),
            pltpu.VMEM((2, 8, 128), f32),
            pltpu.VMEM((VALS * GRID, OCTET), bf16),
            pltpu.VMEM((4, OCTET, GRID), bf16),
            pltpu.VMEM((4, GRID, OCTET), bf16),
            pltpu.VMEM((VALS * GRID, GRID), f32),
            pltpu.VMEM((GRID, 2 * GRID), bf16),
            pltpu.VMEM((NI, HIGH, GRID), bf16),
            pltpu.VMEM((NI, HIGH, GRID), bf16),
            pltpu.VMEM((HIGH, GRID), bf16),
            pltpu.VMEM((2, HIGH, GRID), bf16),
            pltpu.VMEM((2, 8, 128), f32),
            dma((NQ,)),
            dma((NQ,)),
            dma((NZ,)),
            dma((NZ,)),
            dma((NI,)),
            dma((NI,)),
            dma((2,)),
            dma((2,)),
            dma((2, NI)),
            dma((2, NI)),
            dma((2,)),
            dma,
            dma,
            dma((len(given),)),
            pltpu.SemaphoreType.REGULAR((2,)),
        ],
        compiler_params=pltpu.CompilerParams(
            collective_id=1, has_side_effects=True, vmem_limit_bytes=VMEM_LIMIT
        ),
        name="density",
    )(*given)
    return wide(result.reshape(2, GRID, GRID))


def solution(mesh):
    return jax.shard_map(
        shards,
        mesh=mesh,
        in_specs=(P(None, None, ("band", "pw"), None), P(), P(), P(), P(), P("band")),
        out_specs=P("pw", None, None),
        check_vma=False,
    )
```
